32 devices in a mesh: ctx: 16 (over z, x, core), head: 2 (over y).
Axes of the slice: x: 2, y: 2, z: 4, core: 2. Of those that a mesh axis runs over, the one named last changes fastest.
Arguments:
- queries: bfloat16 [16384, 1024], P(('ctx', 'head'))
- keys: bfloat16 [16384, 256], P(('ctx', 'head'))
- values: bfloat16 [16384, 256], P(('ctx', 'head')), may hold values from -6 to 6
- q_feature: bfloat16 [8, 128, 64], P('head'), may hold values from -0.5 to 0.5
- k_feature: bfloat16 [2, 128, 64], P('head'), may hold values from -0.5 to 0.5
- doc_lengths: int32 [64], replicated, may hold values from 1 to 7680, as said below
Outputs:
- attended: bfloat16 [16384, 1024], P('ctx', 'head')
The draws below stay inside these ranges and needn't reach their ends.
Inputs may be any that keep to these rules, and one draw needn't show every extreme that they name: `doc_lengths`: positive lengths that sum to 16384; the first document has length 7680 and the second 3 * 1024.
All inputs are finite; a program needn't handle non-finite values.
Results may differ from the reference program's by a relative error of at most 0.0052.
Values may be sent and summed in bfloat16 or wider, within the bound.
A program may use at most 64 MiB of HBM per device.

```python
import jax
import jax.numpy as jnp
from jax import lax

HD = 128
HALF = 64
T_CTX = 1024
DOCS = 64
KVH = 2
QH = 8
TOKENS = 16384


def draw_queries(key, part):
    shape = (TOKENS, QH * HD)
    base = jnp.clip(jax.random.normal(jax.random.fold_in(key, 1), shape, jnp.float32), -6.0, 6.0)
    return base.astype(jnp.bfloat16)


def draw_keys(key, part):
    shape = (TOKENS, KVH * HD)
    base = jnp.clip(jax.random.normal(jax.random.fold_in(key, 5), shape, jnp.float32), -6.0, 6.0)
    return base.astype(jnp.bfloat16)


def draw_doc_lengths(key, part):
    first_length = TOKENS // 2 - T_CTX // 2
    second_length = 3 * T_CTX
    rest_total = TOKENS - first_length - second_length
    shuffled = jax.random.permutation(jax.random.fold_in(key, 11), rest_total - 1).astype(jnp.int32) + 1
    cut_points = jnp.sort(shuffled[:DOCS - 3])
    bounds = jnp.concatenate([jnp.zeros((1,), jnp.int32), cut_points, jnp.full((1,), rest_total, jnp.int32)])
    rest_lengths = (bounds[1:] - bounds[:-1]).astype(jnp.int32)
    return jnp.concatenate([jnp.full((1,), first_length, jnp.int32), jnp.full((1,), second_length, jnp.int32), rest_lengths]).astype(jnp.int32)


def levels(key, shape, split, smallest, largest):
    loudness, own = 1.0, jax.random.fold_in(key, 6)
    for position, shards_of in split:
        heights = jnp.exp(jax.random.uniform(jax.random.fold_in(own, position), (shards_of,), jnp.float32, smallest / len(split), largest / len(split)))
        loudness = loudness * jnp.repeat(heights, shape[position] // shards_of).reshape([-1 if axis == position else 1 for axis in range(len(shape))])
    return loudness


def scatter_about(rng, dims, scale, bound, cuts=(), held_as=jnp.bfloat16):
    values = scale * jax.random.normal(rng, dims, jnp.float32)
    if cuts:
        values = values * levels(rng, dims, cuts, -0.22, 0.18)
    return jnp.clip(values, -bound, bound).astype(held_as)


def setup_inputs(seed: int = 0) -> dict:
    key_of = jax.random.split(jax.random.key(seed), 7)
    queries = draw_queries(jax.random.fold_in(key_of[6], 71), 0)
    keys = draw_keys(jax.random.fold_in(key_of[6], 71), 0)
    values = scatter_about(key_of[2], (TOKENS, KVH * HD), 1.0, 6.0, ((0, 32),))
    q_feature = scatter_about(key_of[3], (QH, HD, HALF), HD ** -0.5, 0.5, ((0, 2),))
    k_feature = scatter_about(key_of[4], (KVH, HD, HALF), HD ** -0.5, 0.5, ((0, 2),))
    doc_lengths = draw_doc_lengths(jax.random.fold_in(key_of[6], 71), 0)
    return dict(queries=queries, keys=keys, values=values, q_feature=q_feature, k_feature=k_feature, doc_lengths=doc_lengths)


def hedgehog(inputs, weight):
    projected = jnp.einsum("nhd,hdf->nhf", inputs.astype(jnp.float32), weight.astype(jnp.float32))
    return jnp.concatenate([jax.nn.softmax(projected, -1), jax.nn.softmax(-projected, -1)], -1).astype(jnp.bfloat16)


def block_state(phi_k, values, doc_ids):
    last_mask = (doc_ids == doc_ids[-1]).astype(jnp.bfloat16)[:, None]
    chosen = phi_k * last_mask
    state_s = jnp.dot(chosen.T, values, preferred_element_type=jnp.float32)
    state_z = jnp.sum(chosen.astype(jnp.float32), 0)
    return state_s, state_z


def block_output(phi_q, phi_k, values, doc_ids, prev_doc, carry_s, carry_z):
    length = doc_ids.shape[0]
    rows_index = jnp.arange(length)
    causal = (rows_index[None, :] <= rows_index[:, None]) & (doc_ids[:, None] == doc_ids[None, :])
    carried = (doc_ids == prev_doc).astype(jnp.float32)
    results = []
    for head_index in range(phi_q.shape[1]):
        phi_head = phi_q[:, head_index, :]
        scores = jnp.dot(phi_head, phi_k.T, preferred_element_type=jnp.float32)
        masked = jnp.where(causal, scores, 0.0)
        wide_head = phi_head.astype(jnp.float32)
        denominator = jnp.sum(masked, -1) + carried * jnp.dot(wide_head, carry_z, precision=lax.Precision.HIGHEST)
        numerator = jnp.dot(masked.astype(jnp.bfloat16), values, preferred_element_type=jnp.float32)
        numerator = numerator + carried[:, None] * jnp.dot(wide_head, carry_s, precision=lax.Precision.HIGHEST)
        results.append(numerator / denominator[:, None])
    return jnp.stack(results, 1)


def reference(queries, keys, values, q_feature, k_feature, doc_lengths):
    starts = jnp.cumsum(doc_lengths) - doc_lengths
    blocks = TOKENS // T_CTX
    head_size = q_feature.shape[1]
    kv_heads = k_feature.shape[0]
    per_group = q_feature.shape[0] // kv_heads
    feats = 2 * q_feature.shape[2]
    q_blocks = queries.reshape(blocks, T_CTX, -1, head_size)
    k_blocks = keys.reshape(blocks, T_CTX, kv_heads, head_size)
    v_blocks = values.reshape(blocks, T_CTX, kv_heads, head_size)

    def advance(totals, inputs):
        q_here, k_here, v_here, block_index = inputs
        begin = block_index * T_CTX
        positions = begin + jnp.arange(T_CTX).astype(jnp.int32)
        doc_ids = (jnp.sum((starts[None, :] <= positions[:, None]).astype(jnp.int32), 1) - 1).astype(jnp.int32)
        prev_doc = (jnp.sum((starts <= begin - 1).astype(jnp.int32)) - 1).astype(jnp.int32)
        phi_q = hedgehog(q_here, q_feature).reshape(T_CTX, kv_heads, per_group, feats).transpose(1, 0, 2, 3)
        phi_k = hedgehog(k_here, k_feature).transpose(1, 0, 2)
        vals_heads = v_here.transpose(1, 0, 2)
        outputs = jax.vmap(block_output, in_axes=(0, 0, 0, None, None, 0, 0))(phi_q, phi_k, vals_heads, doc_ids, prev_doc, totals[0], totals[1])
        state_s, state_z = jax.vmap(block_state, in_axes=(0, 0, None))(phi_k, vals_heads, doc_ids)
        keep = 1.0 - (doc_ids[-1] != prev_doc).astype(jnp.float32)
        new_totals = (state_s + keep * totals[0], state_z + keep * totals[1])
        return new_totals, outputs.transpose(1, 0, 2, 3).reshape(T_CTX, -1).astype(jnp.bfloat16)

    initial = (jnp.zeros((kv_heads, feats, head_size), jnp.float32), jnp.zeros((kv_heads, feats), jnp.float32))
    indices = jnp.arange(blocks).astype(jnp.int32)
    finals, outputs = lax.scan(advance, initial, (q_blocks, k_blocks, v_blocks, indices))
    return outputs.reshape(TOKENS, -1)
```

```python
import functools

import jax
import jax.numpy as jnp
from jax import lax
from jax.experimental import pallas as pl
from jax.experimental.pallas import tpu as pltpu
from jax.sharding import PartitionSpec as P

MESH = pl.DeviceIdType.MESH
F32 = jnp.float32
BF16 = jnp.bfloat16
NT = (((1,), (1,)), ((), ()))
TN = (((0,), (0,)), ((), ()))
SECOND = 3 * 1024
ZROWS = 16


def iota(shape, dim):
    return lax.broadcasted_iota(jnp.int32, shape, dim)


def feature_map(x, w_ext, pair_sum):
    p = jnp.dot(x, w_ext, preferred_element_type=F32)
    first = iota(p.shape, 1) < p.shape[1] // 2
    top = jnp.max(jnp.where(first, p, -jnp.inf), 1, keepdims=True)
    low = jnp.max(jnp.where(first, -jnp.inf, p), 1, keepdims=True)
    e = jnp.exp(p - jnp.where(first, top, low))
    hi = e.astype(BF16)
    lo = (e - hi.astype(F32)).astype(BF16)
    total = jnp.dot(jnp.concatenate([hi, lo], 1), pair_sum, preferred_element_type=F32)
    return (e / total).astype(BF16)


def kernel(
    n_ctx, n_head, chunk, n0, n1, reach,
    q_hbm, k_hbm, v_hbm, wq_ref, wk_ref, len_ref, out_hbm,
    q_buf, k_buf, v_buf, phi_k, carry, state_out, state_in, out_buf,
    own_sem, kv_send, kv_recv, q_send, q_recv, s_send, s_recv, out_sem,
):
    me, b = lax.axis_index("head"), lax.axis_index("ctx")
    rows = q_hbm.shape[0]
    heads, length, hd = q_buf.shape
    per = rows // chunk
    chunks = length // chunk
    begin = b * length

    def last_of(j):
        return jnp.where(j < n0, n0 - 1, jnp.where(j < n1, n1 - 1, n_ctx - 1))

    def first_of(j):
        return jnp.where(j < n0, 0, jnp.where(j < n1, n0, n1))

    n_to = jnp.minimum(last_of(b) + 1, n_ctx - 1) - b
    n_from = jnp.where(b == 0, 0, b - first_of(b - 1))

    own = pl.ds(pl.multiple_of(me * rows, rows), rows)
    own_cols = pl.ds(pl.multiple_of(me * hd, hd), hd)
    own_copies = [
        pltpu.make_async_copy(k_hbm.at[:, own_cols], k_buf.at[own, :], own_sem.at[0]),
        pltpu.make_async_copy(v_hbm.at[:, own_cols], v_buf.at[own, :], own_sem.at[1]),
    ]
    for h in range(heads):
        cols = pl.ds(pl.multiple_of((me * heads + h) * hd, hd), hd)
        own_copies.append(
            pltpu.make_async_copy(q_hbm.at[:, cols], q_buf.at[h, own, :], own_sem.at[2 + h])
        )
    for c in own_copies:
        c.start()

    barrier = pltpu.get_barrier_semaphore()
    for o in range(1, n_head):
        pl.semaphore_signal(
            barrier, inc=1, device_id=(b, lax.rem(me + o, n_head)), device_id_type=MESH
        )

    def greet(i, _):
        @pl.when(i <= n_to)
        def _():
            pl.semaphore_signal(barrier, inc=1, device_id=(b + i, me), device_id_type=MESH)

        @pl.when(i <= n_from)
        def _():
            pl.semaphore_signal(barrier, inc=1, device_id=(b - i, me), device_id_type=MESH)

        return 0

    lax.fori_loop(1, reach + 1, greet, 0)

    docs = len_ref.shape[1]
    lens = jnp.broadcast_to(len_ref[...].astype(F32), (docs, docs))
    e_i, d_i = iota((docs, docs), 0), iota((docs, docs), 1)
    starts_col = jnp.sum(jnp.where(d_i < e_i, lens, 0.0), 1, keepdims=True)
    starts = jnp.sum(jnp.where(e_i == d_i, starts_col, 0.0), 0, keepdims=True)

    def doc_start(pos):
        return jnp.max(jnp.where(starts <= pos, starts, -1.0), 1, keepdims=True)

    lanes = 2 * hd
    half = hd // 2
    r_i, c_i = lax.rem(iota((lanes, hd), 0), hd), iota((lanes, hd), 1)
    pair_sum = ((r_i < half) == (c_i < half)).astype(F32).astype(BF16)
    ones = jnp.ones((chunk, hd), BF16)

    def widened(w):
        w = w.astype(F32)
        return jnp.concatenate([w, -w], 1).astype(BF16)

    wk = widened(wk_ref[0])
    wq = [widened(wq_ref[h]) for h in range(heads)]

    pl.semaphore_wait(barrier, n_head - 1 + n_to + n_from)

    def kv_copy(o, which):
        to = lax.rem(me + o, n_head)
        cols = pl.ds(pl.multiple_of(to * hd, hd), hd)
        src, dst = ((k_hbm, k_buf), (v_hbm, v_buf))[which]
        return pltpu.make_async_remote_copy(
            src_ref=src.at[:, cols],
            dst_ref=dst.at[own, :],
            send_sem=kv_send.at[o - 1, which],
            recv_sem=kv_recv.at[o - 1, which],
            device_id=(b, to),
            device_id_type=MESH,
        )

    def q_copy(o, i, h):
        to = lax.rem(me + o, n_head)
        cols = pl.ds(pl.multiple_of((to * heads + h) * hd, hd), hd)
        return pltpu.make_async_remote_copy(
            src_ref=q_hbm.at[pl.ds(i * chunk, chunk), cols],
            dst_ref=q_buf.at[h, pl.ds(pl.multiple_of(me * rows + i * chunk, chunk), chunk), :],
            send_sem=q_send.at[o - 1, i, h],
            recv_sem=q_recv.at[o - 1, i, h],
            device_id=(b, to),
            device_id_type=MESH,
        )

    for o in range(1, n_head):
        kv_copy(o, 0).start()
        kv_copy(o, 1).start()
    for o in range(1, n_head):
        for i in range(per):
            for h in range(heads):
                q_copy(o, i, h).start()

    def chunk_rows(c):
        return pl.ds(pl.multiple_of(c * chunk, chunk), chunk)

    def map_keys(c, _):
        phi_k[chunk_rows(c), :] = feature_map(k_buf[chunk_rows(c), :], wk, pair_sum)
        return 0

    def map_queries(c, _):
        for h in range(heads):
            q_buf[h, chunk_rows(c), :] = feature_map(q_buf[h, chunk_rows(c), :], wq[h], pair_sum)
        return 0

    for c in own_copies:
        c.wait()
    lax.fori_loop(me * per, me * per + per, map_keys, 0)
    lax.fori_loop(me * per, me * per + per, map_queries, 0)
    for o in range(1, n_head):
        kv_copy(o, 0).wait_recv()
        kv_copy(o, 1).wait_recv()
        peer = lax.rem(me - o + n_head, n_head)
        lax.fori_loop(peer * per, peer * per + per, map_keys, 0)

    total = jnp.zeros((2 * hd, hd), F32)
    for c in range(chunks):
        carry[c] = total
        c0 = begin + c * chunk
        edge = doc_start((c0 + chunk - 1).astype(F32))
        pos = (c0 + iota((chunk, 1), 0)).astype(F32)
        keys = phi_k[pl.ds(c * chunk, chunk), :]
        chosen = jnp.where(pos >= edge, keys.astype(F32), 0.0).astype(BF16)
        v_ext = jnp.concatenate([v_buf[pl.ds(c * chunk, chunk), :], ones], 1)
        new = lax.dot_general(v_ext, chosen, TN, preferred_element_type=F32)
        total = new + jnp.where(edge < c0.astype(F32), total, 0.0)
    state_out[...] = total[: hd + ZROWS].astype(BF16)

    def s_copy(i):
        return pltpu.make_async_remote_copy(
            src_ref=state_out,
            dst_ref=state_in.at[i - 1],
            send_sem=s_send.at[i - 1],
            recv_sem=s_recv.at[i - 1],
            device_id=(b + i, me),
            device_id_type=MESH,
        )

    def push(i, _):
        @pl.when(i <= n_to)
        def _():
            s_copy(i).start()

        return 0

    lax.fori_loop(1, reach + 1, push, 0)

    before = doc_start((begin - 1).astype(F32))
    state_sum = carry.at[chunks, pl.ds(0, hd + ZROWS), :]
    state_sum[...] = jnp.zeros((hd + ZROWS, hd), F32)

    def collect(i, _):
        @pl.when(i <= n_from)
        def _():
            s_copy(i).wait_recv()
            end = ((b - i + 1) * length - 1).astype(F32)
            state_sum[...] += jnp.where(end >= before, state_in[i - 1].astype(F32), 0.0)

        return 0

    lax.fori_loop(1, reach + 1, collect, 0)
    entering = state_sum[...]
    z_row = entering[hd : hd + 1]
    entering = jnp.concatenate([entering[:hd], jnp.broadcast_to(z_row, (hd, hd))], 0)

    def out_copy(c, h):
        return pltpu.make_async_copy(
            out_buf.at[h, chunk_rows(c), :],
            out_hbm.at[chunk_rows(c), pl.ds(h * hd, hd)],
            out_sem.at[c, h],
        )

    def attend(c, o=None, i=None):
        here = chunk_rows(c)
        c0 = begin + c * chunk
        pos = (c0 + iota((chunk, 1), 0)).astype(F32)
        lo = doc_start(pos)
        s_pos = (c0 + iota((chunk, chunk), 1)).astype(F32)
        mask = (s_pos <= pos) & (s_pos >= lo)
        carried = lo < c0.astype(F32)
        edge = doc_start((c0 - 1).astype(F32))
        held = carry[c] + jnp.where(edge < begin.astype(F32), entering, 0.0)
        held = held.astype(BF16)
        keys = phi_k[here, :]
        v_ext = jnp.concatenate([v_buf[here, :], ones], 1)
        for h in range(heads):
            if o is not None:
                q_copy(o, i, h).wait_recv()
                phi = feature_map(q_buf[h, here, :], wq[h], pair_sum)
            else:
                phi = q_buf[h, here, :]
            scores = lax.dot_general(phi, keys, NT, preferred_element_type=F32)
            weights = jnp.where(mask, scores, 0.0).astype(BF16)
            old = jnp.where(carried, phi.astype(F32), 0.0).astype(BF16)
            acc = jnp.dot(weights, v_ext, preferred_element_type=F32)
            acc += lax.dot_general(old, held, NT, preferred_element_type=F32)
            out_buf[h, here, :] = (acc[:, :hd] / acc[:, hd:]).astype(BF16)
            out_copy(c, h).start()

    def own_chunk(i, _):
        attend(me * per + i)
        return 0

    lax.fori_loop(0, per, own_chunk, 0)
    for o in range(1, n_head):
        peer = lax.rem(me - o + n_head, n_head)

        def peer_chunk(i, _):
            attend(peer * per + i, o, i)
            return 0

        lax.fori_loop(0, per, peer_chunk, 0)

    for o in range(1, n_head):
        kv_copy(o, 0).wait_send()
        kv_copy(o, 1).wait_send()
        for i in range(per):
            for h in range(heads):
                q_copy(o, i, h).wait_send()

    def pushed(i, _):
        @pl.when(i <= n_to)
        def _():
            s_copy(i).wait_send()

        return 0

    lax.fori_loop(1, reach + 1, pushed, 0)
    for c in range(chunks):
        for h in range(heads):
            out_copy(c, h).wait()


def body(n_ctx, n_head, queries, keys, values, q_feature, k_feature, doc_lengths):
    rows = queries.shape[0]
    heads, hd, _ = q_feature.shape
    length = rows * n_head
    tokens = length * n_ctx
    chunk = min(256, rows)
    chunks = length // chunk
    per = rows // chunk
    first = tokens // 2 - length // 2
    n0, n1 = first // length, (first + SECOND) // length
    reach = min(max(n0, n1 - n0, n_ctx - n1), n_ctx - 1)
    any_space = pl.BlockSpec(memory_space=pl.ANY)
    vmem = pl.BlockSpec(memory_space=pltpu.VMEM)
    dma = pltpu.SemaphoreType.DMA
    others = max(n_head - 1, 1)
    return pl.pallas_call(
        functools.partial(kernel, n_ctx, n_head, chunk, n0, n1, reach),
        out_shape=jax.ShapeDtypeStruct((length, heads * hd), BF16),
        in_specs=[any_space] * 3 + [vmem] * 3,
        out_specs=any_space,
        scratch_shapes=[
            pltpu.VMEM((heads, length, hd), BF16),
            pltpu.VMEM((length, hd), BF16),
            pltpu.VMEM((length, hd), BF16),
            pltpu.VMEM((length, hd), BF16),
            pltpu.VMEM((chunks + 1, 2 * hd, hd), F32),
            pltpu.VMEM((hd + ZROWS, hd), BF16),
            pltpu.VMEM((reach, hd + ZROWS, hd), BF16),
            pltpu.VMEM((heads, length, hd), BF16),
            dma((2 + heads,)),
            dma((others, 2)),
            dma((others, 2)),
            dma((others, per, heads)),
            dma((others, per, heads)),
            dma((reach,)),
            dma((reach,)),
            dma((chunks, heads)),
        ],
        compiler_params=pltpu.CompilerParams(
            collective_id=0, has_side_effects=True, vmem_limit_bytes=32 << 20
        ),
    )(queries, keys, values, q_feature, k_feature, doc_lengths.reshape(1, -1))


def solution(mesh):
    placed = (
        P(("ctx", "head"), None),
        P(("ctx", "head"), None),
        P(("ctx", "head"), None),
        P("head", None, None),
        P("head", None, None),
        P(),
    )
    return jax.shard_map(
        functools.partial(body, mesh.shape["ctx"], mesh.shape["head"]),
        mesh=mesh,
        in_specs=placed,
        out_specs=P("ctx", "head"),
        check_vma=False,
    )
```

```python
import functools

import jax
import jax.numpy as jnp
from jax import lax
from jax.experimental import pallas as pl
from jax.experimental.pallas import tpu as pltpu
from jax.sharding import PartitionSpec as P

MESH = pl.DeviceIdType.MESH
F32 = jnp.float32
BF16 = jnp.bfloat16
NT = (((1,), (1,)), ((), ()))
TN = (((0,), (0,)), ((), ()))
SECOND = 3 * 1024
ZROWS = 16


def iota(shape, dim):
    return lax.broadcasted_iota(jnp.int32, shape, dim)


def feature_map(x, w_ext, pair_sum):
    p = lax.dot_general(x, w_ext, NT, preferred_element_type=F32)
    first = iota(p.shape, 1) < p.shape[1] // 2
    top = jnp.max(jnp.where(first, p, -jnp.inf), 1, keepdims=True)
    low = jnp.max(jnp.where(first, -jnp.inf, p), 1, keepdims=True)
    e = jnp.exp(p - jnp.where(first, top, low))
    hi = e.astype(BF16)
    lo = (e - hi.astype(F32)).astype(BF16)
    total = jnp.dot(jnp.concatenate([hi, lo], 1), pair_sum, preferred_element_type=F32)
    return (e / total).astype(BF16)


def kernel(
    n_ctx, n_head, chunk, n0, n1, reach,
    q_hbm, k_hbm, v_hbm, wq_ref, wk_ref, len_ref, out_hbm,
    q_buf, k_buf, v_buf, phi_k, carry, state_out, state_in, out_buf,
    own_sem, kv_send, kv_recv, q_send, q_recv, s_send, s_recv, out_sem,
):
    me, b = lax.axis_index("head"), lax.axis_index("ctx")
    rows = q_hbm.shape[0]
    heads, length, hd = q_buf.shape
    per = rows // chunk
    chunks = length // chunk
    begin = b * length

    def last_of(j):
        return jnp.where(j < n0, n0 - 1, jnp.where(j < n1, n1 - 1, n_ctx - 1))

    def first_of(j):
        return jnp.where(j < n0, 0, jnp.where(j < n1, n0, n1))

    n_to = jnp.minimum(last_of(b) + 1, n_ctx - 1) - b
    n_from = jnp.where(b == 0, 0, b - first_of(b - 1))

    own = pl.ds(pl.multiple_of(me * rows, rows), rows)
    own_cols = pl.ds(pl.multiple_of(me * hd, hd), hd)
    own_copies = [
        pltpu.make_async_copy(k_hbm.at[:, own_cols], k_buf.at[own, :], own_sem.at[0]),
        pltpu.make_async_copy(v_hbm.at[:, own_cols], v_buf.at[own, :], own_sem.at[1]),
    ]
    for h in range(heads):
        cols = pl.ds(pl.multiple_of((me * heads + h) * hd, hd), hd)
        own_copies.append(
            pltpu.make_async_copy(q_hbm.at[:, cols], q_buf.at[h, own, :], own_sem.at[2 + h])
        )
    for c in own_copies:
        c.start()

    barrier = pltpu.get_barrier_semaphore()
    for o in range(1, n_head):
        pl.semaphore_signal(
            barrier, inc=1, device_id=(b, lax.rem(me + o, n_head)), device_id_type=MESH
        )

    def greet(i, _):
        @pl.when(i <= n_to)
        def _():
            pl.semaphore_signal(barrier, inc=1, device_id=(b + i, me), device_id_type=MESH)

        @pl.when(i <= n_from)
        def _():
            pl.semaphore_signal(barrier, inc=1, device_id=(b - i, me), device_id_type=MESH)

        return 0

    lax.fori_loop(1, reach + 1, greet, 0)

    docs = len_ref.shape[1]
    lens = jnp.broadcast_to(len_ref[...].astype(F32), (docs, docs))
    e_i, d_i = iota((docs, docs), 0), iota((docs, docs), 1)
    starts_col = jnp.sum(jnp.where(d_i < e_i, lens, 0.0), 1, keepdims=True)
    starts = jnp.sum(jnp.where(e_i == d_i, starts_col, 0.0), 0, keepdims=True)

    def doc_start(pos):
        return jnp.max(jnp.where(starts <= pos, starts, -1.0), 1, keepdims=True)

    lanes = 2 * hd
    half = hd // 2
    r_i, c_i = lax.rem(iota((lanes, hd), 0), hd), iota((lanes, hd), 1)
    pair_sum = ((r_i < half) == (c_i < half)).astype(F32).astype(BF16)
    ones = jnp.ones((chunk, hd), BF16)

    def widened(w):
        w = w.astype(F32)
        return jnp.concatenate([w, -w], 0).astype(BF16)

    wk = widened(wk_ref[0])
    wq = [widened(wq_ref[h]) for h in range(heads)]

    pl.semaphore_wait(barrier, n_head - 1 + n_to + n_from)

    def kv_copy(o, which):
        to = lax.rem(me + o, n_head)
        cols = pl.ds(pl.multiple_of(to * hd, hd), hd)
        src, dst = ((k_hbm, k_buf), (v_hbm, v_buf))[which]
        return pltpu.make_async_remote_copy(
            src_ref=src.at[:, cols],
            dst_ref=dst.at[own, :],
            send_sem=kv_send.at[o - 1, which],
            recv_sem=kv_recv.at[o - 1, which],
            device_id=(b, to),
            device_id_type=MESH,
        )

    def q_copy(o, i, h):
        to = lax.rem(me + o, n_head)
        cols = pl.ds(pl.multiple_of((to * heads + h) * hd, hd), hd)
        return pltpu.make_async_remote_copy(
            src_ref=q_hbm.at[pl.ds(i * chunk, chunk), cols],
            dst_ref=q_buf.at[h, pl.ds(pl.multiple_of(me * rows + i * chunk, chunk), chunk), :],
            send_sem=q_send.at[o - 1, i, h],
            recv_sem=q_recv.at[o - 1, i, h],
            device_id=(b, to),
            device_id_type=MESH,
        )

    for o in range(1, n_head):
        kv_copy(o, 0).start()
        kv_copy(o, 1).start()
    for o in range(1, n_head):
        for i in range(per):
            for h in range(heads):
                q_copy(o, i, h).start()

    def chunk_rows(c):
        return pl.ds(pl.multiple_of(c * chunk, chunk), chunk)

    def map_keys(c, _):
        phi_k[chunk_rows(c), :] = feature_map(k_buf[chunk_rows(c), :], wk, pair_sum)
        return 0

    def map_queries(c, _):
        for h in range(heads):
            q_buf[h, chunk_rows(c), :] = feature_map(q_buf[h, chunk_rows(c), :], wq[h], pair_sum)
        return 0

    for c in own_copies:
        c.wait()
    lax.fori_loop(me * per, me * per + per, map_keys, 0)
    lax.fori_loop(me * per, me * per + per, map_queries, 0)
    for o in range(1, n_head):
        kv_copy(o, 0).wait_recv()
        kv_copy(o, 1).wait_recv()
        peer = lax.rem(me - o + n_head, n_head)
        lax.fori_loop(peer * per, peer * per + per, map_keys, 0)

    total = jnp.zeros((2 * hd, hd), F32)
    for c in range(chunks):
        carry[c] = total
        c0 = begin + c * chunk
        edge = doc_start((c0 + chunk - 1).astype(F32))
        pos = (c0 + iota((chunk, 1), 0)).astype(F32)
        keys = phi_k[pl.ds(c * chunk, chunk), :]
        chosen = jnp.where(pos >= edge, keys.astype(F32), 0.0).astype(BF16)
        v_ext = jnp.concatenate([v_buf[pl.ds(c * chunk, chunk), :], ones], 1)
        new = lax.dot_general(v_ext, chosen, TN, preferred_element_type=F32)
        total = new + jnp.where(edge < c0.astype(F32), total, 0.0)
    state_out[...] = total[: hd + ZROWS].astype(BF16)

    def s_copy(i):
        return pltpu.make_async_remote_copy(
            src_ref=state_out,
            dst_ref=state_in.at[i - 1],
            send_sem=s_send.at[i - 1],
            recv_sem=s_recv.at[i - 1],
            device_id=(b + i, me),
            device_id_type=MESH,
        )

    def push(i, _):
        @pl.when(i <= n_to)
        def _():
            s_copy(i).start()

        return 0

    lax.fori_loop(1, reach + 1, push, 0)

    before = doc_start((begin - 1).astype(F32))
    state_sum = carry.at[chunks, pl.ds(0, hd + ZROWS), :]
    state_sum[...] = jnp.zeros((hd + ZROWS, hd), F32)

    def collect(i, _):
        @pl.when(i <= n_from)
        def _():
            s_copy(i).wait_recv()
            end = ((b - i + 1) * length - 1).astype(F32)
            state_sum[...] += jnp.where(end >= before, state_in[i - 1].astype(F32), 0.0)

        return 0

    lax.fori_loop(1, reach + 1, collect, 0)
    entering = state_sum[...]
    z_row = entering[hd : hd + 1]
    entering = jnp.concatenate([entering[:hd], jnp.broadcast_to(z_row, (hd, hd))], 0)

    def out_copy(c, h):
        return pltpu.make_async_copy(
            out_buf.at[h, chunk_rows(c), :],
            out_hbm.at[chunk_rows(c), pl.ds(h * hd, hd)],
            out_sem.at[c, h],
        )

    def attend(c, o=None, i=None):
        here = chunk_rows(c)
        c0 = begin + c * chunk
        pos = (c0 + iota((chunk, 1), 0)).astype(F32)
        lo = doc_start(pos)
        s_pos = (c0 + iota((chunk, chunk), 1)).astype(F32)
        mask = (s_pos <= pos) & (s_pos >= lo)
        carried = lo < c0.astype(F32)
        edge = doc_start((c0 - 1).astype(F32))
        held = carry[c] + jnp.where(edge < begin.astype(F32), entering, 0.0)
        held = held.astype(BF16)
        keys = phi_k[here, :]
        v_ext = jnp.concatenate([v_buf[here, :], ones], 1)
        for h in range(heads):
            if o is not None:
                q_copy(o, i, h).wait_recv()
                phi = feature_map(q_buf[h, here, :], wq[h], pair_sum)
            else:
                phi = q_buf[h, here, :]
            scores = lax.dot_general(phi, keys, NT, preferred_element_type=F32)
            weights = jnp.where(mask, scores, 0.0).astype(BF16)
            old = jnp.where(carried, phi.astype(F32), 0.0).astype(BF16)
            acc = jnp.dot(weights, v_ext, preferred_element_type=F32)
            acc += lax.dot_general(old, held, NT, preferred_element_type=F32)
            out_buf[h, here, :] = (acc[:, :hd] / acc[:, hd:]).astype(BF16)
            out_copy(c, h).start()

    def own_chunk(i, _):
        attend(me * per + i)
        return 0

    lax.fori_loop(0, per, own_chunk, 0)
    for o in range(1, n_head):
        peer = lax.rem(me - o + n_head, n_head)

        def peer_chunk(i, _):
            attend(peer * per + i, o, i)
            return 0

        lax.fori_loop(0, per, peer_chunk, 0)

    for o in range(1, n_head):
        kv_copy(o, 0).wait_send()
        kv_copy(o, 1).wait_send()
        for i in range(per):
            for h in range(heads):
                q_copy(o, i, h).wait_send()

    def pushed(i, _):
        @pl.when(i <= n_to)
        def _():
            s_copy(i).wait_send()

        return 0

    lax.fori_loop(1, reach + 1, pushed, 0)
    for c in range(chunks):
        for h in range(heads):
            out_copy(c, h).wait()


def body(n_ctx, n_head, queries, keys, values, q_feature, k_feature, doc_lengths):
    rows = queries.shape[0]
    heads, hd, _ = q_feature.shape
    length = rows * n_head
    tokens = length * n_ctx
    chunk = min(256, rows)
    chunks = length // chunk
    per = rows // chunk
    first = tokens // 2 - length // 2
    n0, n1 = first // length, (first + SECOND) // length
    reach = min(max(n0, n1 - n0, n_ctx - n1), n_ctx - 1)
    hbm = pl.BlockSpec(memory_space=pltpu.HBM)
    vmem = pl.BlockSpec(memory_space=pltpu.VMEM)
    dma = pltpu.SemaphoreType.DMA
    others = max(n_head - 1, 1)
    return pl.pallas_call(
        functools.partial(kernel, n_ctx, n_head, chunk, n0, n1, reach),
        out_shape=jax.ShapeDtypeStruct((length, heads * hd), BF16),
        in_specs=[hbm] * 3 + [vmem] * 3,
        out_specs=hbm,
        scratch_shapes=[
            pltpu.VMEM((heads, length, hd), BF16),
            pltpu.VMEM((length, hd), BF16),
            pltpu.VMEM((length, hd), BF16),
            pltpu.VMEM((length, hd), BF16),
            pltpu.VMEM((chunks + 1, 2 * hd, hd), F32),
            pltpu.VMEM((hd + ZROWS, hd), BF16),
            pltpu.VMEM((reach, hd + ZROWS, hd), BF16),
            pltpu.VMEM((heads, length, hd), BF16),
            dma((2 + heads,)),
            dma((others, 2)),
            dma((others, 2)),
            dma((others, per, heads)),
            dma((others, per, heads)),
            dma((reach,)),
            dma((reach,)),
            dma((chunks, heads)),
        ],
        compiler_params=pltpu.CompilerParams(
            collective_id=0, has_side_effects=True, vmem_limit_bytes=60 << 20
        ),
    )(queries, keys, values, q_feature.transpose(0, 2, 1), k_feature.transpose(0, 2, 1), doc_lengths.reshape(1, -1))


def solution(mesh):
    placed = (
        P(("ctx", "head"), None),
        P(("ctx", "head"), None),
        P(("ctx", "head"), None),
        P("head", None, None),
        P("head", None, None),
        P(),
    )
    return jax.shard_map(
        functools.partial(body, mesh.shape["ctx"], mesh.shape["head"]),
        mesh=mesh,
        in_specs=placed,
        out_specs=P("ctx", "head"),
        check_vma=False,
    )
```

```python
import functools

import jax
import jax.numpy as jnp
from jax import lax
from jax.experimental import pallas as pl
from jax.experimental.pallas import tpu as pltpu
from jax.sharding import PartitionSpec as P

MESH = pl.DeviceIdType.MESH
F32 = jnp.float32
BF16 = jnp.bfloat16
NT = (((1,), (1,)), ((), ()))
TN = (((0,), (0,)), ((), ()))
SECOND = 3 * 1024
ZROWS = 16


def iota(shape, dim):
    return lax.broadcasted_iota(jnp.int32, shape, dim)


def feature_map(x, w_ext, pair_sum):
    p = lax.dot_general(x, w_ext, NT, preferred_element_type=F32)
    first = iota(p.shape, 1) < p.shape[1] // 2
    top = jnp.max(jnp.where(first, p, -jnp.inf), 1, keepdims=True)
    low = jnp.max(jnp.where(first, -jnp.inf, p), 1, keepdims=True)
    e = jnp.exp(p - jnp.where(first, top, low))
    hi = e.astype(BF16)
    lo = (e - hi.astype(F32)).astype(BF16)
    total = jnp.dot(jnp.concatenate([hi, lo], 1), pair_sum, preferred_element_type=F32)
    return (e / total).astype(BF16)


def kernel(
    n_ctx, n_head, chunk, n0, n1, reach,
    q_hbm, k_hbm, v_hbm, wq_hbm, wk_hbm, len_hbm, out_ref,
    q_buf, k_buf, v_buf, phi_k, carry, state_out, state_in,
    wq_ref, wk_ref, len_ref,
    small_sem, own_sem, kv_send, kv_recv, q_send, q_recv, s_send, s_recv,
):
    me, b = lax.axis_index("head"), lax.axis_index("ctx")
    rows = q_hbm.shape[0]
    heads, length, hd = q_buf.shape
    per = rows // chunk
    chunks = length // chunk
    begin = b * length

    def last_of(j):
        return jnp.where(j < n0, n0 - 1, jnp.where(j < n1, n1 - 1, n_ctx - 1))

    def first_of(j):
        return jnp.where(j < n0, 0, jnp.where(j < n1, n0, n1))

    n_to = jnp.minimum(last_of(b) + 1, n_ctx - 1) - b
    n_from = jnp.where(b == 0, 0, b - first_of(b - 1))

    small = [
        pltpu.make_async_copy(src, dst, small_sem.at[i])
        for i, (src, dst) in enumerate(
            ((len_hbm, len_ref), (wk_hbm, wk_ref), (wq_hbm, wq_ref))
        )
    ]
    for c in small:
        c.start()

    own = pl.ds(pl.multiple_of(me * rows, rows), rows)
    own_cols = pl.ds(pl.multiple_of(me * hd, hd), hd)
    own_copies = [
        pltpu.make_async_copy(k_hbm.at[:, own_cols], k_buf.at[own, :], own_sem.at[0]),
        pltpu.make_async_copy(v_hbm.at[:, own_cols], v_buf.at[own, :], own_sem.at[1]),
    ]
    for h in range(heads):
        cols = pl.ds(pl.multiple_of((me * heads + h) * hd, hd), hd)
        own_copies.append(
            pltpu.make_async_copy(q_hbm.at[:, cols], q_buf.at[h, own, :], own_sem.at[2 + h])
        )
    for c in own_copies:
        c.start()

    barrier = pltpu.get_barrier_semaphore()
    for o in range(1, n_head):
        pl.semaphore_signal(
            barrier, inc=1, device_id=(b, lax.rem(me + o, n_head)), device_id_type=MESH
        )

    def greet(i, _):
        @pl.when(i <= n_to)
        def _():
            pl.semaphore_signal(barrier, inc=1, device_id=(b + i, me), device_id_type=MESH)

        @pl.when(i <= n_from)
        def _():
            pl.semaphore_signal(barrier, inc=1, device_id=(b - i, me), device_id_type=MESH)

        return 0

    lax.fori_loop(1, reach + 1, greet, 0)

    for c in small:
        c.wait()
    docs = len_ref.shape[1]
    lens = jnp.broadcast_to(len_ref[...].astype(F32), (docs, docs))
    e_i, d_i = iota((docs, docs), 0), iota((docs, docs), 1)
    starts_col = jnp.sum(jnp.where(d_i < e_i, lens, 0.0), 1, keepdims=True)
    starts = jnp.sum(jnp.where(e_i == d_i, starts_col, 0.0), 0, keepdims=True)

    def doc_start(pos):
        return jnp.max(jnp.where(starts <= pos, starts, -1.0), 1, keepdims=True)

    lanes = 2 * hd
    half = hd // 2
    r_i, c_i = lax.rem(iota((lanes, hd), 0), hd), iota((lanes, hd), 1)
    pair_sum = ((r_i < half) == (c_i < half)).astype(F32).astype(BF16)
    ones = jnp.ones((chunk, hd), BF16)

    def widened(w):
        w = w.astype(F32)
        return jnp.concatenate([w, -w], 0).astype(BF16)

    wk = widened(wk_ref[0])
    wq = [widened(wq_ref[h]) for h in range(heads)]

    pl.semaphore_wait(barrier, n_head - 1 + n_to + n_from)

    def kv_copy(o, which):
        to = lax.rem(me + o, n_head)
        cols = pl.ds(pl.multiple_of(to * hd, hd), hd)
        src, dst = ((k_hbm, k_buf), (v_hbm, v_buf))[which]
        return pltpu.make_async_remote_copy(
            src_ref=src.at[:, cols],
            dst_ref=dst.at[own, :],
            send_sem=kv_send.at[o - 1, which],
            recv_sem=kv_recv.at[o - 1, which],
            device_id=(b, to),
            device_id_type=MESH,
        )

    def q_copy(o, i, h):
        to = lax.rem(me + o, n_head)
        cols = pl.ds(pl.multiple_of((to * heads + h) * hd, hd), hd)
        return pltpu.make_async_remote_copy(
            src_ref=q_hbm.at[pl.ds(i * chunk, chunk), cols],
            dst_ref=q_buf.at[h, pl.ds(pl.multiple_of(me * rows + i * chunk, chunk), chunk), :],
            send_sem=q_send.at[o - 1, i, h],
            recv_sem=q_recv.at[o - 1, i, h],
            device_id=(b, to),
            device_id_type=MESH,
        )

    for o in range(1, n_head):
        kv_copy(o, 0).start()
        kv_copy(o, 1).start()
    for o in range(1, n_head):
        for i in range(per):
            for h in range(heads):
                q_copy(o, i, h).start()

    def chunk_rows(c):
        return pl.ds(pl.multiple_of(c * chunk, chunk), chunk)

    def map_keys(c, _):
        phi_k[chunk_rows(c), :] = feature_map(k_buf[chunk_rows(c), :], wk, pair_sum)
        return 0

    def map_queries(c, _):
        for h in range(heads):
            q_buf[h, chunk_rows(c), :] = feature_map(q_buf[h, chunk_rows(c), :], wq[h], pair_sum)
        return 0

    for c in own_copies:
        c.wait()
    lax.fori_loop(me * per, me * per + per, map_keys, 0)
    lax.fori_loop(me * per, me * per + per, map_queries, 0)
    for o in range(1, n_head):
        kv_copy(o, 0).wait_recv()
        kv_copy(o, 1).wait_recv()
        peer = lax.rem(me - o + n_head, n_head)
        lax.fori_loop(peer * per, peer * per + per, map_keys, 0)

    total = jnp.zeros((2 * hd, hd), F32)
    for c in range(chunks):
        carry[c] = total
        c0 = begin + c * chunk
        edge = doc_start((c0 + chunk - 1).astype(F32))
        pos = (c0 + iota((chunk, 1), 0)).astype(F32)
        keys = phi_k[pl.ds(c * chunk, chunk), :]
        chosen = jnp.where(pos >= edge, keys.astype(F32), 0.0).astype(BF16)
        v_ext = jnp.concatenate([v_buf[pl.ds(c * chunk, chunk), :], ones], 1)
        new = lax.dot_general(v_ext, chosen, TN, preferred_element_type=F32)
        total = new + jnp.where(edge < c0.astype(F32), total, 0.0)
    state_out[...] = total[: hd + ZROWS].astype(BF16)

    def s_copy(i):
        return pltpu.make_async_remote_copy(
            src_ref=state_out,
            dst_ref=state_in.at[i - 1],
            send_sem=s_send.at[i - 1],
            recv_sem=s_recv.at[i - 1],
            device_id=(b + i, me),
            device_id_type=MESH,
        )

    def push(i, _):
        @pl.when(i <= n_to)
        def _():
            s_copy(i).start()

        return 0

    lax.fori_loop(1, reach + 1, push, 0)

    before = doc_start((begin - 1).astype(F32))
    state_sum = carry.at[chunks, pl.ds(0, hd + ZROWS), :]
    state_sum[...] = jnp.zeros((hd + ZROWS, hd), F32)

    def collect(i, _):
        @pl.when(i <= n_from)
        def _():
            s_copy(i).wait_recv()
            end = ((b - i + 1) * length - 1).astype(F32)
            state_sum[...] += jnp.where(end >= before, state_in[i - 1].astype(F32), 0.0)

        return 0

    lax.fori_loop(1, reach + 1, collect, 0)
    entering = state_sum[...]
    z_row = entering[hd : hd + 1]
    entering = jnp.concatenate([entering[:hd], jnp.broadcast_to(z_row, (hd, hd))], 0)

    def attend(c, o=None, i=None):
        here = chunk_rows(c)
        c0 = begin + c * chunk
        pos = (c0 + iota((chunk, 1), 0)).astype(F32)
        lo = doc_start(pos)
        s_pos = (c0 + iota((chunk, chunk), 1)).astype(F32)
        mask = (s_pos <= pos) & (s_pos >= lo)
        carried = lo < c0.astype(F32)
        edge = doc_start((c0 - 1).astype(F32))
        held = carry[c] + jnp.where(edge < begin.astype(F32), entering, 0.0)
        held = held.astype(BF16)
        keys = phi_k[here, :]
        v_ext = jnp.concatenate([v_buf[here, :], ones], 1)
        for h in range(heads):
            if o is not None:
                q_copy(o, i, h).wait_recv()
                phi = feature_map(q_buf[h, here, :], wq[h], pair_sum)
            else:
                phi = q_buf[h, here, :]
            scores = lax.dot_general(phi, keys, NT, preferred_element_type=F32)
            weights = jnp.where(mask, scores, 0.0).astype(BF16)
            old = jnp.where(carried, phi.astype(F32), 0.0).astype(BF16)
            acc = jnp.dot(weights, v_ext, preferred_element_type=F32)
            acc += lax.dot_general(old, held, NT, preferred_element_type=F32)
            out_ref[here, h * hd : (h + 1) * hd] = (acc[:, :hd] / acc[:, hd:]).astype(BF16)

    def own_chunk(i, _):
        attend(me * per + i)
        return 0

    lax.fori_loop(0, per, own_chunk, 0)
    for o in range(1, n_head):
        peer = lax.rem(me - o + n_head, n_head)

        def peer_chunk(i, _):
            attend(peer * per + i, o, i)
            return 0

        lax.fori_loop(0, per, peer_chunk, 0)

    for o in range(1, n_head):
        kv_copy(o, 0).wait_send()
        kv_copy(o, 1).wait_send()
        for i in range(per):
            for h in range(heads):
                q_copy(o, i, h).wait_send()

    def pushed(i, _):
        @pl.when(i <= n_to)
        def _():
            s_copy(i).wait_send()

        return 0

    lax.fori_loop(1, reach + 1, pushed, 0)


def body(n_ctx, n_head, queries, keys, values, q_feature, k_feature, doc_lengths):
    rows = queries.shape[0]
    heads, hd, _ = q_feature.shape
    length = rows * n_head
    tokens = length * n_ctx
    chunk = min(256, rows)
    chunks = length // chunk
    per = rows // chunk
    first = tokens // 2 - length // 2
    n0, n1 = first // length, (first + SECOND) // length
    reach = min(max(n0, n1 - n0, n_ctx - n1), n_ctx - 1)
    hbm = pl.BlockSpec(memory_space=pltpu.HBM)
    vmem = pl.BlockSpec(memory_space=pltpu.VMEM)
    dma = pltpu.SemaphoreType.DMA
    others = max(n_head - 1, 1)
    operands = (
        queries, keys, values,
        q_feature.transpose(0, 2, 1), k_feature.transpose(0, 2, 1),
        doc_lengths.reshape(1, -1),
    )
    return pl.pallas_call(
        functools.partial(kernel, n_ctx, n_head, chunk, n0, n1, reach),
        out_shape=jax.ShapeDtypeStruct((length, heads * hd), BF16),
        in_specs=[hbm] * 6,
        out_specs=vmem,
        scratch_shapes=[
            pltpu.VMEM((heads, length, hd), BF16),
            pltpu.VMEM((length, hd), BF16),
            pltpu.VMEM((length, hd), BF16),
            pltpu.VMEM((length, hd), BF16),
            pltpu.VMEM((chunks + 1, 2 * hd, hd), F32),
            pltpu.VMEM((hd + ZROWS, hd), BF16),
            pltpu.VMEM((reach, hd + ZROWS, hd), BF16),
            pltpu.VMEM((heads, hd // 2, hd), BF16),
            pltpu.VMEM((1, hd // 2, hd), BF16),
            pltpu.VMEM((1, doc_lengths.shape[0]), jnp.int32),
            dma((3,)),
            dma((2 + heads,)),
            dma((others, 2)),
            dma((others, 2)),
            dma((others, per, heads)),
            dma((others, per, heads)),
            dma((reach,)),
            dma((reach,)),
        ],
        compiler_params=pltpu.CompilerParams(
            collective_id=0, has_side_effects=True, vmem_limit_bytes=32 << 20
        ),
    )(*[pltpu.with_memory_space_constraint(a, pltpu.HBM) for a in operands])


def solution(mesh):
    placed = (
        P(("ctx", "head"), None),
        P(("ctx", "head"), None),
        P(("ctx", "head"), None),
        P("head", None, None),
        P("head", None, None),
        P(),
    )
    return jax.shard_map(
        functools.partial(body, mesh.shape["ctx"], mesh.shape["head"]),
        mesh=mesh,
        in_specs=placed,
        out_specs=P("ctx", "head"),
        check_vma=False,
    )
```

```python
import functools

import jax
import jax.numpy as jnp
from jax import lax
from jax.experimental import pallas as pl
from jax.experimental.pallas import tpu as pltpu
from jax.sharding import PartitionSpec as P

MESH = pl.DeviceIdType.MESH
F32 = jnp.float32
BF16 = jnp.bfloat16
NT = (((1,), (1,)), ((), ()))
TN = (((0,), (0,)), ((), ()))
SECOND = 3 * 1024
ZROWS = 16


def iota(shape, dim):
    return lax.broadcasted_iota(jnp.int32, shape, dim)


def feature_map(x, w_ext, pair_sum):
    p = lax.dot_general(x, w_ext, NT, preferred_element_type=F32)
    first = iota(p.shape, 1) < p.shape[1] // 2
    top = jnp.max(jnp.where(first, p, -jnp.inf), 1, keepdims=True)
    low = jnp.max(jnp.where(first, -jnp.inf, p), 1, keepdims=True)
    e = jnp.exp(p - jnp.where(first, top, low))
    hi = e.astype(BF16)
    lo = (e - hi.astype(F32)).astype(BF16)
    total = jnp.dot(jnp.concatenate([hi, lo], 1), pair_sum, preferred_element_type=F32)
    return (e / total).astype(BF16)


def kernel(
    n_ctx, n_head, chunk, n0, n1, reach,
    q_hbm, k_hbm, v_hbm, wq_hbm, wk_hbm, len_hbm, out_ref,
    q_buf, k_buf, v_buf, phi_k, carry, state_out, state_in,
    wq_ref, wk_ref, len_ref,
    small_sem, own_sem, kv_send, kv_recv, q_send, q_recv, s_send, s_recv,
):
    me, b = lax.axis_index("head"), lax.axis_index("ctx")
    rows = q_hbm.shape[0]
    heads, length, hd = q_buf.shape
    per = rows // chunk
    chunks = length // chunk
    begin = b * length

    def last_of(j):
        return jnp.where(j < n0, n0 - 1, jnp.where(j < n1, n1 - 1, n_ctx - 1))

    def first_of(j):
        return jnp.where(j < n0, 0, jnp.where(j < n1, n0, n1))

    n_to = jnp.minimum(last_of(b) + 1, n_ctx - 1) - b
    n_from = jnp.where(b == 0, 0, b - first_of(b - 1))

    small = [
        pltpu.make_async_copy(src, dst, small_sem.at[i])
        for i, (src, dst) in enumerate(
            ((len_hbm, len_ref), (wk_hbm, wk_ref), (wq_hbm, wq_ref))
        )
    ]
    for c in small:
        c.start()

    own = pl.ds(pl.multiple_of(me * rows, rows), rows)
    own_cols = pl.ds(pl.multiple_of(me * hd, hd), hd)
    own_copies = [
        pltpu.make_async_copy(k_hbm.at[:, own_cols], k_buf.at[own, :], own_sem.at[0]),
        pltpu.make_async_copy(v_hbm.at[:, own_cols], v_buf.at[own, :], own_sem.at[1]),
    ]
    for h in range(heads):
        cols = pl.ds(pl.multiple_of((me * heads + h) * hd, hd), hd)
        own_copies.append(
            pltpu.make_async_copy(q_hbm.at[:, cols], q_buf.at[h, own, :], own_sem.at[2 + h])
        )
    for c in own_copies:
        c.start()

    barrier = pltpu.get_barrier_semaphore()
    for o in range(1, n_head):
        pl.semaphore_signal(
            barrier, inc=1, device_id=(b, lax.rem(me + o, n_head)), device_id_type=MESH
        )

    def greet(i, _):
        @pl.when(i <= n_to)
        def _():
            pl.semaphore_signal(barrier, inc=1, device_id=(b + i, me), device_id_type=MESH)

        @pl.when(i <= n_from)
        def _():
            pl.semaphore_signal(barrier, inc=1, device_id=(b - i, me), device_id_type=MESH)

        return 0

    lax.fori_loop(1, reach + 1, greet, 0)

    for c in small:
        c.wait()
    docs = len_ref.shape[1]
    lens = jnp.broadcast_to(len_ref[...].astype(F32), (docs, docs))
    e_i, d_i = iota((docs, docs), 0), iota((docs, docs), 1)
    starts_col = jnp.sum(jnp.where(d_i < e_i, lens, 0.0), 1, keepdims=True)
    starts = jnp.sum(jnp.where(e_i == d_i, starts_col, 0.0), 0, keepdims=True)

    def doc_start(pos):
        return jnp.max(jnp.where(starts <= pos, starts, -1.0), 1, keepdims=True)

    lanes = 2 * hd
    half = hd // 2
    r_i, c_i = lax.rem(iota((lanes, hd), 0), hd), iota((lanes, hd), 1)
    pair_sum = ((r_i < half) == (c_i < half)).astype(F32).astype(BF16)
    ones = jnp.ones((chunk, hd), BF16)

    def widened(w):
        w = w.astype(F32)
        return jnp.concatenate([w, -w], 0).astype(BF16)

    wk = widened(wk_ref[0])
    wq = [widened(wq_ref[h]) for h in range(heads)]

    pl.semaphore_wait(barrier, n_head - 1 + n_to + n_from)

    def kv_copy(o, which):
        to = lax.rem(me + o, n_head)
        cols = pl.ds(pl.multiple_of(to * hd, hd), hd)
        src, dst = ((k_hbm, k_buf), (v_hbm, v_buf))[which]
        return pltpu.make_async_remote_copy(
            src_ref=src.at[:, cols],
            dst_ref=dst.at[own, :],
            send_sem=kv_send.at[o - 1, which],
            recv_sem=kv_recv.at[o - 1, which],
            device_id=(b, to),
            device_id_type=MESH,
        )

    def q_copy(o, i, h):
        to = lax.rem(me + o, n_head)
        cols = pl.ds(pl.multiple_of((to * heads + h) * hd, hd), hd)
        return pltpu.make_async_remote_copy(
            src_ref=q_hbm.at[pl.ds(i * chunk, chunk), cols],
            dst_ref=q_buf.at[h, pl.ds(pl.multiple_of(me * rows + i * chunk, chunk), chunk), :],
            send_sem=q_send.at[o - 1, i, h],
            recv_sem=q_recv.at[o - 1, i, h],
            device_id=(b, to),
            device_id_type=MESH,
        )

    for o in range(1, n_head):
        kv_copy(o, 0).start()
        kv_copy(o, 1).start()
    for o in range(1, n_head):
        for i in range(per):
            for h in range(heads):
                q_copy(o, i, h).start()

    def chunk_rows(c):
        return pl.ds(pl.multiple_of(c * chunk, chunk), chunk)

    def map_keys(c, _):
        phi_k[chunk_rows(c), :] = feature_map(k_buf[chunk_rows(c), :], wk, pair_sum)
        return 0

    def map_queries(c, _):
        for h in range(heads):
            q_buf[h, chunk_rows(c), :] = feature_map(q_buf[h, chunk_rows(c), :], wq[h], pair_sum)
        return 0

    for c in own_copies:
        c.wait()
    lax.fori_loop(me * per, me * per + per, map_keys, 0)
    lax.fori_loop(me * per, me * per + per, map_queries, 0)
    for o in range(1, n_head):
        kv_copy(o, 0).wait_recv()
        kv_copy(o, 1).wait_recv()
        peer = lax.rem(me - o + n_head, n_head)
        lax.fori_loop(peer * per, peer * per + per, map_keys, 0)

    total = jnp.zeros((2 * hd, hd), F32)
    for c in range(chunks):
        carry[c] = total
        c0 = begin + c * chunk
        edge = doc_start((c0 + chunk - 1).astype(F32))
        pos = (c0 + iota((chunk, 1), 0)).astype(F32)
        keys = phi_k[pl.ds(c * chunk, chunk), :]
        chosen = jnp.where(pos >= edge, keys.astype(F32), 0.0).astype(BF16)
        v_ext = jnp.concatenate([v_buf[pl.ds(c * chunk, chunk), :], ones], 1)
        new = lax.dot_general(v_ext, chosen, TN, preferred_element_type=F32)
        total = new + jnp.where(edge < c0.astype(F32), total, 0.0)
    state_out[...] = total[: hd + ZROWS].astype(BF16)

    def s_copy(i):
        return pltpu.make_async_remote_copy(
            src_ref=state_out,
            dst_ref=state_in.at[i - 1],
            send_sem=s_send.at[i - 1],
            recv_sem=s_recv.at[i - 1],
            device_id=(b + i, me),
            device_id_type=MESH,
        )

    def push(i, _):
        @pl.when(i <= n_to)
        def _():
            s_copy(i).start()

        return 0

    lax.fori_loop(1, reach + 1, push, 0)

    before = doc_start((begin - 1).astype(F32))
    state_sum = carry.at[chunks, pl.ds(0, hd + ZROWS), :]
    state_sum[...] = jnp.zeros((hd + ZROWS, hd), F32)

    def collect(i, _):
        @pl.when(i <= n_from)
        def _():
            s_copy(i).wait_recv()
            end = ((b - i + 1) * length - 1).astype(F32)
            state_sum[...] += jnp.where(end >= before, state_in[i - 1].astype(F32), 0.0)

        return 0

    lax.fori_loop(1, reach + 1, collect, 0)
    entering = state_sum[...]
    z_row = entering[hd : hd + 1]
    entering = jnp.concatenate([entering[:hd], jnp.broadcast_to(z_row, (hd, hd))], 0)

    def attend(c, o=None, i=None):
        here = chunk_rows(c)
        c0 = begin + c * chunk
        pos = (c0 + iota((chunk, 1), 0)).astype(F32)
        lo = doc_start(pos)
        s_pos = (c0 + iota((chunk, chunk), 1)).astype(F32)
        mask = (s_pos <= pos) & (s_pos >= lo)
        carried = lo < c0.astype(F32)
        edge = doc_start((c0 - 1).astype(F32))
        held = carry[c] + jnp.where(edge < begin.astype(F32), entering, 0.0)
        held = held.astype(BF16)
        keys = phi_k[here, :]
        v_ext = jnp.concatenate([v_buf[here, :], ones], 1)
        for h in range(heads):
            if o is not None:
                q_copy(o, i, h).wait_recv()
                phi = feature_map(q_buf[h, here, :], wq[h], pair_sum)
            else:
                phi = q_buf[h, here, :]
            scores = lax.dot_general(phi, keys, NT, preferred_element_type=F32)
            weights = jnp.where(mask, scores, 0.0).astype(BF16)
            old = jnp.where(carried, phi.astype(F32), 0.0).astype(BF16)
            acc = jnp.dot(weights, v_ext, preferred_element_type=F32)
            acc += lax.dot_general(old, held, NT, preferred_element_type=F32)
            out_ref[here, h * hd : (h + 1) * hd] = (acc[:, :hd] / acc[:, hd:]).astype(BF16)

    def own_chunk(i, _):
        attend(me * per + i)
        return 0

    lax.fori_loop(0, per, own_chunk, 0)
    for o in range(1, n_head):
        peer = lax.rem(me - o + n_head, n_head)

        def peer_chunk(i, _):
            attend(peer * per + i, o, i)
            return 0

        lax.fori_loop(0, per, peer_chunk, 0)

    for o in range(1, n_head):
        kv_copy(o, 0).wait_send()
        kv_copy(o, 1).wait_send()
        for i in range(per):
            for h in range(heads):
                q_copy(o, i, h).wait_send()

    def pushed(i, _):
        @pl.when(i <= n_to)
        def _():
            s_copy(i).wait_send()

        return 0

    lax.fori_loop(1, reach + 1, pushed, 0)


def body(n_ctx, n_head, queries, keys, values, q_feature, k_feature, doc_lengths):
    rows = queries.shape[0]
    heads, hd, _ = q_feature.shape
    length = rows * n_head
    tokens = length * n_ctx
    chunk = min(512, rows)
    chunks = length // chunk
    per = rows // chunk
    first = tokens // 2 - length // 2
    n0, n1 = first // length, (first + SECOND) // length
    reach = min(max(n0, n1 - n0, n_ctx - n1), n_ctx - 1)
    hbm = pl.BlockSpec(memory_space=pltpu.HBM)
    vmem = pl.BlockSpec(memory_space=pltpu.VMEM)
    dma = pltpu.SemaphoreType.DMA
    others = max(n_head - 1, 1)
    operands = (
        queries, keys, values,
        q_feature.transpose(0, 2, 1), k_feature.transpose(0, 2, 1),
        doc_lengths.reshape(1, -1),
    )
    return pl.pallas_call(
        functools.partial(kernel, n_ctx, n_head, chunk, n0, n1, reach),
        out_shape=jax.ShapeDtypeStruct((length, heads * hd), BF16),
        in_specs=[hbm] * 6,
        out_specs=vmem,
        scratch_shapes=[
            pltpu.VMEM((heads, length, hd), BF16),
            pltpu.VMEM((length, hd), BF16),
            pltpu.VMEM((length, hd), BF16),
            pltpu.VMEM((length, hd), BF16),
            pltpu.VMEM((chunks + 1, 2 * hd, hd), F32),
            pltpu.VMEM((hd + ZROWS, hd), BF16),
            pltpu.VMEM((reach, hd + ZROWS, hd), BF16),
            pltpu.VMEM((heads, hd // 2, hd), BF16),
            pltpu.VMEM((1, hd // 2, hd), BF16),
            pltpu.VMEM((1, doc_lengths.shape[0]), jnp.int32),
            dma((3,)),
            dma((2 + heads,)),
            dma((others, 2)),
            dma((others, 2)),
            dma((others, per, heads)),
            dma((others, per, heads)),
            dma((reach,)),
            dma((reach,)),
        ],
        compiler_params=pltpu.CompilerParams(
            collective_id=0, has_side_effects=True, vmem_limit_bytes=32 << 20
        ),
    )(*[pltpu.with_memory_space_constraint(a, pltpu.HBM) for a in operands])


def solution(mesh):
    placed = (
        P(("ctx", "head"), None),
        P(("ctx", "head"), None),
        P(("ctx", "head"), None),
        P("head", None, None),
        P("head", None, None),
        P(),
    )
    return jax.shard_map(
        functools.partial(body, mesh.shape["ctx"], mesh.shape["head"]),
        mesh=mesh,
        in_specs=placed,
        out_specs=P("ctx", "head"),
        check_vma=False,
    )
```
